32 devices in a mesh: chan: 8 (over z, y), facet: 4 (over x, core).
Axes of the slice: x: 2, y: 2, z: 4, core: 2. Of those that a mesh axis runs over, the one named last changes fastest.
Arguments:
- solution: float32 [8, 2048, 2048], P('chan', 'facet'), may hold values from -6 to 6
- residual: float32 [8, 2048, 2048], P('chan', 'facet'), may hold values from -120 to 120
- direction: float32 [8, 2048, 2048], P('chan', 'facet'), may hold values from -120 to 120
- spectra: float32 [8, 4096, 4096], P('chan', None, 'facet'), may hold values from 0.05 to 1
- basis: float32 [8, 8], replicated, may hold values from -2 to 2
- slot_channel: int32 [8], replicated, may hold values from 0 to 7, each once
Outputs:
- new_solution: float32 [8, 2048, 2048], P('chan', 'facet')
- new_residual: float32 [8, 2048, 2048], P('chan', 'facet')
- new_direction: float32 [8, 2048, 2048], P('chan', 'facet')
The draws below stay inside these ranges and needn't reach their ends.
Inputs may be any that keep to these rules, and one draw needn't show every extreme that they name: `slot_channel`: every channel appears in exactly one slot.
All inputs are finite; a program needn't handle non-finite values.
Results may differ from the reference program's by a relative error of at most 0.000064.
Values sent between devices are 32-bit elements; how exact they have to be, the bound alone decides.
A program may use at most 256 MiB of HBM per device.

```python
import math
import jax
import jax.numpy as jnp
from jax import lax

L = 4096
RANK = 8
N = 2048
CHANNELS = 8


def scaled_cube(key):
    noise_key, row_key, col_key = jax.random.split(key, 3)
    cube_shape = (CHANNELS, N, N)
    noise_values = jax.random.truncated_normal(noise_key, -4.0, 4.0, cube_shape, jnp.float32)
    row_place = jnp.arange(N, dtype=jnp.float32) / (N - 1)
    row_scale = jnp.exp(math.log(3.0) * row_place + math.log(10.0 / 3.0) * jax.random.uniform(row_key, (N,), jnp.float32))
    col_scale = jnp.exp(math.log(10.0) * jax.random.uniform(col_key, (N,), jnp.float32))
    chan_place = jnp.arange(CHANNELS, dtype=jnp.float32) / (CHANNELS - 1)
    chan_scale = jnp.exp(math.log(3.0) * chan_place)
    return noise_values * chan_scale[:, None, None] * row_scale[None, :, None] * col_scale[None, None, :] * 0.1


def draw_residual(key, part):
    return scaled_cube(jax.random.fold_in(key, 11))


def draw_direction(key, part):
    return scaled_cube(jax.random.fold_in(key, 23))


def steps_of(own_key, shape, cuts, smallest, high):
    factor_of = 1.0
    for position, shards_of in cuts:
        heights = jax.random.uniform(jax.random.fold_in(jax.random.fold_in(own_key, 6), position), (shards_of,), jnp.float32, smallest / len(cuts), high / len(cuts))
        factor_of = factor_of * jnp.repeat(jnp.exp(heights), shape[position] // shards_of).reshape((-1,) + (1,) * (len(shape) - 1 - position))
    return factor_of


def centred(key, shape, width, reach, pieces=(), held_as=jnp.bfloat16):
    gain = steps_of(key, shape, pieces, -0.22, 0.18) if pieces else 1.0
    entries = jax.random.normal(key, shape, jnp.float32) * width * gain
    return jnp.minimum(jnp.maximum(entries, -reach), reach).astype(held_as)


def setup_inputs(seed: int = 0) -> dict:
    arg_keys = jax.random.split(jax.random.key(seed), 7)
    solution = centred(arg_keys[0], (CHANNELS, N, N), 1.0, 6.0, ((0, 8), (1, 4)), jnp.float32)
    residual = draw_residual(jax.random.fold_in(arg_keys[6], 71), 0)
    direction = draw_direction(jax.random.fold_in(arg_keys[6], 71), 0)
    spectra = jnp.clip(jnp.exp(math.log(1.0) - 2.9957323 * jax.random.uniform(arg_keys[3], (CHANNELS, L, L), jnp.float32) ** steps_of(arg_keys[3], (CHANNELS, L, L), ((0, 8), (2, 4)), -0.2, 0.2)), 0.05, 1.0)
    basis = centred(arg_keys[4], (CHANNELS, RANK), CHANNELS ** -0.5, 2.0, (), jnp.float32)
    slot_channel = jax.random.permutation(arg_keys[5], CHANNELS).astype(jnp.int32)
    return dict(solution=solution, residual=residual, direction=direction, spectra=spectra, basis=basis, slot_channel=slot_channel)


PRIOR_FLOOR = 0.25


def convolve(planes, spectrum):
    padded = jnp.pad(planes, ((0, L - N), (0, L - N)))
    freqs = jnp.fft.fft2(padded)
    inverse = jnp.real(jnp.fft.ifft2(freqs * spectrum))
    return inverse[:N, :N].astype(planes.dtype)


def reference(solution, residual, direction, spectra, basis, slot_channel):
    blurred = lax.map(lambda pair_in: convolve(pair_in[0], pair_in[1]), (direction, spectra))
    loadings = basis[slot_channel.astype(jnp.int32)]
    coeffs = jnp.einsum("cq,cij->qij", loadings, direction, precision=lax.Precision.HIGHEST)
    applied = blurred + PRIOR_FLOOR * direction + jnp.einsum("cq,qij->cij", loadings, coeffs, precision=lax.Precision.HIGHEST)
    norm_now = jnp.sum(residual * residual)
    curvature = jnp.sum(direction * applied)
    step_size = norm_now / curvature
    new_solution = solution + step_size * direction
    new_residual = residual - step_size * applied
    norm_next = jnp.sum(new_residual * new_residual)
    new_direction = new_residual + (norm_next / norm_now) * direction
    return (new_solution, new_residual, new_direction)
```

```python
import math

import jax
import jax.numpy as jnp
from jax import lax
from jax.sharding import PartitionSpec as P

ROOT = 64


HIGH = lax.Precision.HIGH
HIGHEST = lax.Precision.HIGHEST
PRIOR_FLOOR = 0.25


def wave(product, length, direction_sign):
    angles = (product % length).astype(jnp.float32) * (2.0 * math.pi / length)
    return (jnp.cos(angles), direction_sign * jnp.sin(angles))


def span(size):
    return jnp.arange(size, dtype=jnp.int32)


def swap_pairs(array, count, bit):
    pairs = [(place, place ^ bit) for place in range(count)]
    return lax.ppermute(array, "facet", pairs)


def column_table(width, columns, length, first_column):
    column = first_column + span(columns)[None, :]
    coarse = width // ROOT
    coarse_real, coarse_imag = wave(span(coarse)[:, None] * ROOT * column, length, -1.0)
    fine_real, fine_imag = wave(span(ROOT)[:, None] * column, length, -1.0)
    coarse_real, coarse_imag = (coarse_real[:, None], coarse_imag[:, None])
    fine_real, fine_imag = (fine_real[None], fine_imag[None])
    table_real = (coarse_real * fine_real - coarse_imag * fine_imag).reshape(width, columns)
    table_imag = (coarse_real * fine_imag + coarse_imag * fine_real).reshape(width, columns)
    return lax.optimization_barrier((table_real, table_imag))


def complex_stack(real, imag):
    return jnp.stack([jnp.stack([real, imag]), jnp.stack([-imag, real])])


def row_spectrum_pass(planes, spectrum, row_digits, factor):
    halved, columns = (row_digits.shape[0], planes.shape[2])
    blocks = planes.reshape(2, halved, factor, columns)
    first = complex_stack(*wave(row_digits[:, None] * span(factor)[None, :], factor, -1.0))
    section = jnp.einsum("pjnc,pqjk->kqnc", blocks, first, precision=HIGH)
    spread = span(factor)[:, None, None] * span(factor)[None, :, None] + (
        span(factor)[None, :, None] * span(factor)[None, None, :] * factor
    )
    second = complex_stack(*wave(spread, factor * factor, -1.0))
    freqs = jnp.einsum("kpnc,pqknj->kqjc", section, second, precision=HIGH)
    spectrum = spectrum.reshape(factor, factor, columns).transpose(1, 0, 2)
    weighted = freqs * spectrum[:, None]
    third = complex_stack(*wave(spread, factor * factor, 1.0))
    section = jnp.einsum("kpjc,pqknj->kqnc", weighted, third, precision=HIGH)
    last = complex_stack(*wave(row_digits[:, None] * span(factor)[None, :], factor, 1.0))
    rows = jnp.einsum("kpnc,pqjk->qjnc", section, last, precision=HIGH)
    return rows.reshape(2, halved * factor, columns)


def body(solution, residual, direction, spectra, basis, slot_channel):
    channel_count = basis.shape[0]
    factor = ROOT
    length = factor * factor
    facets = lax.axis_size("facet")
    place = lax.axis_index("facet")
    height, width = direction.shape[1:]
    columns = spectra.shape[2]
    own = direction[0]

    blocks = {0: own}
    bit = facets // 2
    while bit:
        blocks.update({key ^ bit: swap_pairs(blocks[key], facets, bit) for key in list(blocks)})
        bit //= 2
    table_real, table_imag = column_table(width, columns, length, place * columns)

    near = [blocks[key] for key in range(facets // 2)]
    far = [blocks[key] for key in range(facets // 2, facets)]
    near_rows = jnp.concatenate(near, axis=0)
    far_rows = jnp.concatenate(far, axis=0)
    planes = jnp.stack(
        [
            jnp.concatenate(
                [jnp.dot(part, table, precision=HIGH) for part in (near_rows, far_rows)], axis=0
            )
            for table in (table_real, table_imag)
        ]
    )
    digits = height // factor
    row_digits = ((place ^ span(facets))[:, None] * digits + span(digits)[None, :]).reshape(-1)
    rows = row_spectrum_pass(planes, spectra[0], row_digits, factor)

    def partial(part):
        wide = (((1,), (1,)), ((), ()))
        return lax.dot_general(part[0], table_real, wide, precision=HIGH) + lax.dot_general(
            part[1], table_imag, wide, precision=HIGH
        )

    sums = {}
    half = facets // 2
    for base in (half, 0):
        image = partial(rows[:, base * height : (base + half) * height])
        for key in range(half):
            sums[base + key] = image[key * height : (key + 1) * height]
    bit = 1
    while bit < facets:
        sums = {
            key: sums[key] + swap_pairs(sums[key | bit], facets, bit)
            for key in sorted(sums, reverse=True)
            if not key & bit
        }
        bit *= 2
    blurred = sums[0][None] * (1.0 / float(length * length))

    regrouped = lax.all_to_all(direction, "chan", split_axis=1, concat_axis=0, tiled=True)
    one_hot = (slot_channel[:, None] == span(channel_count)[None, :]).astype(jnp.float32)
    loadings = jnp.dot(one_hot, basis, precision=HIGHEST)
    coeffs = jnp.einsum("cq,cij->qij", loadings, regrouped, precision=HIGHEST)
    local_prior = PRIOR_FLOOR * regrouped + jnp.einsum(
        "cq,qij->cij", loadings, coeffs, precision=HIGHEST
    )
    prior_term = lax.all_to_all(local_prior, "chan", split_axis=0, concat_axis=1, tiled=True)
    applied = blurred + prior_term
    moments = jnp.stack(
        [
            jnp.sum(residual * residual),
            jnp.sum(direction * applied),
            jnp.sum(residual * applied),
            jnp.sum(applied * applied),
        ]
    )
    norm_now, curvature, cross, square = lax.psum(moments, ("chan", "facet"))
    step_size = norm_now / curvature
    new_solution = solution + step_size * direction
    new_residual = residual - step_size * applied
    norm_next = norm_now - 2.0 * step_size * cross + step_size * step_size * square
    new_direction = new_residual + norm_next / norm_now * direction
    return (new_solution, new_residual, new_direction)


def solution(mesh):
    return jax.shard_map(
        body,
        mesh=mesh,
        in_specs=(
            P("chan", "facet", None),
            P("chan", "facet", None),
            P("chan", "facet", None),
            P("chan", None, "facet"),
            P(),
            P(),
        ),
        out_specs=(P("chan", "facet", None), P("chan", "facet", None), P("chan", "facet", None)),
        check_vma=False,
    )
```
